32 devices in a mesh: seq: 4 (over y, x), fsdp: 8 (over z, core).
Axes of the slice: x: 2, y: 2, z: 4, core: 2. Of those that a mesh axis runs over, the one named last changes fastest.
Arguments:
- tokens: bfloat16 [8, 512, 2048], P('fsdp', 'seq'), may hold values from -6 to 6
- documents: int32 [8, 512], P('fsdp'), may hold values from 0 to 3, never falling along the last dimension, each value on 1 to 256 neighbouring positions
- cotangent: bfloat16 [8, 512, 2048], P('fsdp', 'seq'), may hold values from -6 to 6
- w_query: bfloat16 [2048, 2048], P('fsdp'), may hold values from -2.5 to 2.5
- w_key: bfloat16 [2048, 512], P('fsdp'), may hold values from -1 to 1
- w_value: bfloat16 [2048, 512], P('fsdp'), may hold values from -0.125 to 0.125
- w_output: bfloat16 [2048, 2048], P('fsdp'), may hold values from -0.5 to 0.5
- w_gate: bfloat16 [2048, 8192], P('fsdp'), may hold values from -0.125 to 0.125
- w_up: bfloat16 [2048, 8192], P('fsdp'), may hold values from -0.125 to 0.125
- w_down: bfloat16 [8192, 2048], P('fsdp'), may hold values from -0.0625 to 0.0625
- gain_attn: bfloat16 [2048], P('fsdp'), may hold values from 0.25 to 1.75
- gain_mlp: bfloat16 [2048], P('fsdp'), may hold values from 0.25 to 1.75
Outputs:
- output: bfloat16 [8, 512, 2048], P('fsdp', 'seq')
- grad_tokens: bfloat16 [8, 512, 2048], P('fsdp', 'seq')
- grad_w_query: float32 [2048, 2048], P('fsdp')
- grad_w_key: float32 [2048, 512], P('fsdp')
- grad_w_value: float32 [2048, 512], P('fsdp')
- grad_w_output: float32 [2048, 2048], P('fsdp')
- grad_w_gate: float32 [2048, 8192], P('fsdp')
- grad_w_up: float32 [2048, 8192], P('fsdp')
- grad_w_down: float32 [8192, 2048], P('fsdp')
- grad_gain_attn: float32 [2048], P('fsdp')
- grad_gain_mlp: float32 [2048], P('fsdp')
The draws below stay inside these ranges and needn't reach their ends.
Inputs may be any that keep to these rules, and one draw needn't show every extreme that they name: Each sequence holds 4 documents numbered in order, each of 1 to 256 tokens, one exactly 256 long.
All inputs are finite; a program needn't handle non-finite values.
Results may differ from the reference program's by a relative error of at most 0.02.
Values may be sent and summed in bfloat16 or wider, within the bound.
No kernel may reach another device: no remote copies, remote signals or barrier semaphores. Data moves between devices by JAX's collectives and lax.ppermute only.
A program may use at most 512 MiB of HBM per device.

```python
import math
import jax
import jax.numpy as jnp
import numpy as np
from jax import lax

D = 2048
HQ = 32
KV = 8
HD = 64
FF = 8192
DOCS = 4
SEQ_LEN = 512
SEQS = 8


def shared_keys(key):
    return jnp.clip(jax.random.normal(jax.random.fold_in(key, 11), (D, KV * HD), jnp.float32), -6.0, 6.0) * D ** (-0.5)


def draw_w_key(key, part):
    return shared_keys(key).astype(jnp.bfloat16)


def draw_w_query(key, part):
    fresh = jnp.clip(jax.random.normal(jax.random.fold_in(key, 13), (D, HQ * HD), jnp.float32), -6.0, 6.0) * D ** (-0.5)
    return fresh.astype(jnp.bfloat16)


def block_scale(key, extent, split, least, high):
    gain, own = 1.0, jax.random.fold_in(key, 6)
    for axis_at, blocks in split:
        draws = jnp.exp(jax.random.uniform(jax.random.fold_in(own, axis_at), (blocks,), jnp.float32, least / len(split), high / len(split)))
        gain = gain * jnp.repeat(draws, extent[axis_at] // blocks).reshape([-1 if axis == axis_at else 1 for axis in range(len(extent))])
    return gain


def split_up(number_of, total, most, slope):
    portions = [(1 << 20) // math.isqrt(standing ** slope) + 1 for standing in range(2, number_of + 1)]
    surplus, holding = total - most - (number_of - 1), [1] * (number_of - 1)
    while surplus > 0:
        movable = [i for i in range(number_of - 1) if holding[i] < most]
        mass, budget = sum([portions[i] for i in movable]), surplus
        for i in movable:
            more = min(most - holding[i], max(1, budget * portions[i] // mass), surplus)
            holding[i] = holding[i] + more
            surplus = surplus - more
    return np.array([most] + holding)


def uneven(stream_key, count, total, limit, slope):
    if count == 2:
        one = jax.random.randint(stream_key, (), max(1, total - limit), min(limit, total - 1) + 1)
        return jnp.stack([one, total - one])
    sizes = jnp.asarray(split_up(count, total, limit, slope), jnp.int32)
    couples = (count - 1) // 2
    donor, taker = sizes[1:1 + 2 * couples:2], sizes[2:2 + 2 * couples:2]
    room = jnp.minimum(donor - 1, limit - taker)
    passed = jax.random.randint(jax.random.fold_in(stream_key, 1), (couples,), 0, 1 << 20) % (room + 1)
    sizes = sizes.at[1:1 + 2 * couples:2].set(donor - passed).at[2:2 + 2 * couples:2].set(taker + passed)
    return sizes[jax.random.permutation(jax.random.fold_in(stream_key, 2), count)]


def noise(stream_key, extent, deviation, reach, split=(), held_as=jnp.bfloat16):
    values = deviation * jax.random.normal(stream_key, extent, jnp.float32)
    if split:
        values = values * block_scale(stream_key, extent, split, -0.22, 0.18)
    return jnp.clip(values, -reach, reach).astype(held_as)


def setup_inputs(seed: int = 0) -> dict:
    splits = jax.random.split(jax.random.key(seed), 13)
    tokens = noise(splits[0], (SEQS, SEQ_LEN, D), 1.0, 6.0, ((0, 8), (1, 4)))
    documents = jax.vmap(lambda own: jnp.searchsorted(jnp.cumsum(uneven(own, DOCS, SEQ_LEN, SEQ_LEN // 2, 1)), jnp.arange(SEQ_LEN), side="right"))(jax.random.split(splits[1], SEQS)).reshape((SEQS, SEQ_LEN)).astype(jnp.int32)
    cotangent = noise(splits[2], (SEQS, SEQ_LEN, D), 1.0, 6.0, ((0, 8), (1, 4)))
    w_query = draw_w_query(jax.random.fold_in(splits[12], 71), 0)
    w_key = draw_w_key(jax.random.fold_in(splits[12], 71), 0)
    w_value = noise(splits[5], (D, KV * HD), D ** -0.5, 0.125, ((0, 8),))
    w_output = noise(splits[6], (HQ * HD, D), (HQ * HD // 16) ** -0.5, 0.5, ((0, 8),))
    w_gate = noise(splits[7], (D, FF), D ** -0.5, 0.125, ((0, 8),))
    w_up = noise(splits[8], (D, FF), D ** -0.5, 0.125, ((0, 8),))
    w_down = noise(splits[9], (FF, D), FF ** -0.5, 0.0625, ((0, 8),))
    gain_attn = jnp.clip(1.0 + 0.15 * jax.random.normal(splits[10], (D,), jnp.float32), 0.25, 1.75).astype(jnp.bfloat16)
    gain_mlp = jnp.clip(1.0 + 0.15 * jax.random.normal(splits[11], (D,), jnp.float32), 0.25, 1.75).astype(jnp.bfloat16)
    return dict(tokens=tokens, documents=documents, cotangent=cotangent, w_query=w_query, w_key=w_key, w_value=w_value, w_output=w_output, w_gate=w_gate, w_up=w_up, w_down=w_down, gain_attn=gain_attn, gain_mlp=gain_mlp)


EPSILON = 1e-05
NEGATIVE = -1e+30
HIGHEST = lax.Precision.HIGHEST

@jax.custom_vjp
def low(v):
    return lax.optimization_barrier(v.astype(jnp.bfloat16)).astype(jnp.float32)

@jax.custom_vjp
def low_back(v):
    return v

def low_keep(v):
    return (low(v), None)

def low_pass(kept, grad):
    return (grad,)

def back_keep(v):
    return (v, None)

def back_low(kept, grad):
    return (low(grad),)
low.defvjp(low_keep, low_pass)
low_back.defvjp(back_keep, back_low)

def frequencies():
    base_rate = 500000.0 ** (-jnp.arange(0, HD, 2, dtype=jnp.float32) / HD)
    wavelength = 2.0 * math.pi / base_rate
    smooth = (8192.0 / wavelength - 1.0) / 3.0
    middle_rate = (1.0 - smooth) * base_rate / 32.0 + smooth * base_rate
    return jnp.where(wavelength > 8192.0, base_rate / 32.0, jnp.where(wavelength < 2048.0, base_rate, middle_rate))

def positions(doc_ids):
    index_all = jnp.arange(doc_ids.shape[0], dtype=jnp.int32)
    fresh = jnp.concatenate([jnp.ones((1,), dtype=bool), doc_ids[1:] != doc_ids[:-1]])
    first_index = lax.cummax(jnp.where(fresh, index_all, jnp.zeros_like(index_all)), axis=0)
    return index_all - first_index

def tables(pos_values):
    angles = pos_values.astype(jnp.float32)[:, None] * frequencies()[None, :]
    return (jnp.concatenate([jnp.cos(angles)] * 2, axis=1), jnp.concatenate([jnp.sin(angles)] * 2, axis=1))

def rotation(values, cosine_table, sine_table):
    row_count = values.shape[0]
    shaped = values.reshape(row_count, -1, HD)
    half_size = HD // 2
    turned = jnp.concatenate([-shaped[..., half_size:], shaped[..., :half_size]], axis=-1)
    return (shaped * cosine_table[:, None, :] + turned * sine_table[:, None, :]).reshape(row_count, -1)

def matrix(left_side, right_side):
    return jnp.dot(left_side, right_side, precision=HIGHEST)

def rescale(values):
    return values * lax.rsqrt(lax.optimization_barrier(jnp.mean(values * values, axis=-1, keepdims=True)) + EPSILON)

def attend(queries, keys_all, values_all, doc_ids):
    length = queries.shape[0]
    group_size = HQ // KV
    index_all = jnp.arange(length, dtype=jnp.int32)
    visible = (index_all[None, :] <= index_all[:, None]) & (doc_ids[:, None] == doc_ids[None, :])
    query_groups = jnp.transpose(queries.reshape(length, KV, group_size, HD), (1, 0, 2, 3))
    key_groups = jnp.transpose(keys_all.reshape(length, KV, HD), (1, 0, 2))
    value_groups = jnp.transpose(values_all.reshape(length, KV, HD), (1, 0, 2))

    def one_group(element):
        query_head, key_head, value_head = element
        scores = low_back(jnp.einsum('qgd,kd->gqk', query_head, key_head, precision=HIGHEST) * HD ** (-0.5))
        scores = jnp.where(visible[None], scores, NEGATIVE)
        largest = lax.optimization_barrier(jnp.max(scores, axis=-1, keepdims=True))
        expo = jnp.exp(scores - largest)
        probs = expo / lax.optimization_barrier(jnp.sum(expo, axis=-1, keepdims=True))
        return jnp.einsum('gqk,kd->qgd', low(probs), value_head, precision=HIGHEST)
    mixed_groups = lax.map(jax.checkpoint(one_group), (query_groups, key_groups, value_groups))
    return jnp.transpose(mixed_groups, (1, 0, 2, 3)).reshape(length, HQ * HD)

def layer(params, inputs, doc_ids):
    w_query, w_key, w_value, w_output, w_gate, w_up, w_down, gain_attn, gain_mlp = params
    cosine_table, sine_table = tables(positions(doc_ids))
    normed = low(rescale(inputs) * gain_attn)
    queries = low_back(low(rotation(low_back(matrix(normed, w_query)), cosine_table, sine_table)))
    keys_all = low_back(low(rotation(low_back(matrix(normed, w_key)), cosine_table, sine_table)))
    values_all = low_back(low(matrix(normed, w_value)))
    mixed = low_back(low(attend(queries, keys_all, values_all, doc_ids)))
    middle = inputs + low_back(matrix(mixed, w_output))
    normed_two = low(rescale(middle) * gain_mlp)
    gate = low_back(matrix(normed_two, w_gate))
    upward = low_back(matrix(normed_two, w_up))
    hidden = low(gate * jax.nn.sigmoid(gate) * upward)
    return middle + low_back(matrix(hidden, w_down))

def reference(tokens, documents, cotangent, w_query, w_key, w_value, w_output, w_gate, w_up, w_down, gain_attn, gain_mlp):
    weights = tuple((element.astype(jnp.float32) for element in (w_query, w_key, w_value, w_output, w_gate, w_up, w_down, gain_attn, gain_mlp)))

    def one_sequence(totals, element):
        inputs, doc_ids, upstream = element
        result, pullback = jax.vjp(lambda params, values: layer(params, values, doc_ids), weights, inputs.astype(jnp.float32))
        grads, input_grad = pullback(upstream.astype(jnp.float32))
        totals = jax.tree.map(jnp.add, totals, grads)
        return (totals, (result.astype(jnp.bfloat16), input_grad.astype(jnp.bfloat16)))
    zero_totals = jax.tree.map(jnp.zeros_like, weights)
    totals, outputs = lax.scan(one_sequence, zero_totals, (tokens, documents, cotangent))
    return (outputs[0], outputs[1], totals[0], totals[1], totals[2], totals[3], totals[4], totals[5], totals[6], totals[7], totals[8])
```

```python
import math

import jax
import jax.numpy as jnp
from jax import lax
from jax.sharding import Mesh
from jax.sharding import PartitionSpec as P

HD = 64
EPSILON = 1e-05
NEGATIVE = -1e30
SEQ = ("sa", "sb")
FS = ("p", "q", "c")
F32 = jnp.float32
BF16 = jnp.bfloat16


def frequencies():
    base_rate = 500000.0 ** (-jnp.arange(0, HD, 2, dtype=F32) / HD)
    wavelength = 2.0 * math.pi / base_rate
    smooth = (8192.0 / wavelength - 1.0) / 3.0
    middle_rate = (1.0 - smooth) * base_rate / 32.0 + smooth * base_rate
    return jnp.where(
        wavelength > 8192.0,
        base_rate / 32.0,
        jnp.where(wavelength < 2048.0, base_rate, middle_rate),
    )


def positions(doc_ids):
    index_all = jnp.arange(doc_ids.shape[0], dtype=jnp.int32)
    fresh = jnp.concatenate([jnp.ones((1,), dtype=bool), doc_ids[1:] != doc_ids[:-1]])
    first_index = lax.cummax(jnp.where(fresh, index_all, jnp.zeros_like(index_all)), axis=0)
    return index_all - first_index


def tables(pos_values):
    angles = pos_values.astype(F32)[:, None] * frequencies()[None, :]
    return (
        jnp.concatenate([jnp.cos(angles)] * 2, axis=1),
        jnp.concatenate([jnp.sin(angles)] * 2, axis=1),
    )


def rotation(values, cosine_table, sine_table):
    row_count = values.shape[0]
    shaped = values.reshape(row_count, -1, HD)
    half_size = HD // 2
    turned = jnp.concatenate([-shaped[..., half_size:], shaped[..., :half_size]], axis=-1)
    return (shaped * cosine_table[:, None, :] + turned * sine_table[:, None, :]).reshape(
        row_count, -1
    )


def product(left_side, right_side):
    return jnp.dot(left_side, right_side, preferred_element_type=F32)


def product_back(left_side, right_side):
    return lax.dot_general(
        left_side, right_side, (((1,), (1,)), ((), ())), preferred_element_type=F32
    )


def outer_rows(left_side, right_side):
    return lax.dot_general(
        left_side, right_side, (((0,), (0,)), ((), ())), preferred_element_type=F32
    )


def norm_factor(values):
    return lax.rsqrt(jnp.mean(values * values, axis=-1, keepdims=True) + EPSILON)


def norm_back(grad_normed, normed, factor):
    return factor * (grad_normed - normed * jnp.mean(grad_normed * normed, axis=-1, keepdims=True))


def swap(value, axes, size, distance):
    return lax.ppermute(value, axes, [(i, i ^ distance) for i in range(size)])


def low(value):
    return value.astype(BF16)


def layer_step(seq_size, fs_size):
    pairs = fs_size // 4

    def seq_swap(value, distance):
        return swap(value, SEQ, seq_size, distance)

    def gather_seq(block):
        if seq_size == 4:
            half = block.shape[0] // 2
            one, two = seq_swap(block, 1), seq_swap(block, 2)
            far = [seq_swap(two[:half], 1), seq_swap(one[half:], 2)]
            return [block, one, two, jnp.concatenate(far)]
        blocks, distance = [block], 1
        while distance < seq_size:
            got = seq_swap(jnp.stack(blocks), distance)
            blocks = blocks + [got[i] for i in range(distance)]
            distance *= 2
        return blocks

    def scatter_seq(blocks):
        if seq_size == 4:
            half = blocks[0].shape[0] // 2
            near, one, two, far = blocks
            far_low = low(far)
            to_two = seq_swap(far_low[:half], 1)
            to_one = seq_swap(far_low[half:], 2)
            one_top = seq_swap(low(one[:half]), 1)
            two_end = seq_swap(low(two[half:]), 2)
            one_end = seq_swap(low(one[half:].astype(F32) + to_one.astype(F32)), 1)
            two_top = seq_swap(low(two[:half].astype(F32) + to_two.astype(F32)), 2)
            return near.astype(F32) + jnp.concatenate(
                [
                    one_top.astype(F32) + two_top.astype(F32),
                    one_end.astype(F32) + two_end.astype(F32),
                ]
            )
        distance = seq_size // 2
        while distance:
            got = seq_swap(low(jnp.stack(blocks[distance:])), distance).astype(F32)
            blocks = [blocks[i].astype(F32) + got[i] for i in range(distance)]
            distance //= 2
        return blocks[0]

    def sum_all(value):
        for axes, size in ((FS, fs_size), (SEQ, seq_size)):
            distance = 1
            while distance < size:
                value = value + swap(value, axes, size, distance)
                distance *= 2
        return value

    def shards(
        tokens,
        documents,
        cotangent,
        w_query,
        w_key,
        w_value,
        w_output,
        w_gate,
        w_up,
        w_down,
        gain_attn,
        gain_mlp,
    ):
        rows, width = tokens.shape[1], tokens.shape[2]
        hidden_width = w_gate.shape[1]
        length = rows * seq_size
        own_seq = lax.axis_index(SEQ)
        own_fs = lax.axis_index(FS)

        def own_columns(weight):
            part = weight.shape[1] // seq_size
            return lax.dynamic_slice_in_dim(weight, own_seq * part, part, 1)

        def relative(blocks):
            return jnp.concatenate(
                [
                    lax.dynamic_index_in_dim(blocks, own_seq ^ k, 0, keepdims=True)
                    for k in range(seq_size)
                ]
            )

        tokens_own = tokens.reshape(rows, width)
        cot_own = cotangent.reshape(rows, width)
        doc_ids = documents.reshape(-1)
        token_blocks = gather_seq(tokens_own)
        attn_in = jnp.concatenate(
            [own_columns(w_query), own_columns(w_key), own_columns(w_value)], axis=1
        )
        full_qkv = lax.all_gather(attn_in, FS, axis=0, tiled=True)
        q_cols = w_query.shape[1] // seq_size
        k_cols = w_key.shape[1] // seq_size
        gains = jnp.stack([gain_attn, gain_mlp])
        gain_blocks, distance = gains[None], 1
        while distance < fs_size:
            gain_blocks = jnp.concatenate(
                [gain_blocks, swap(gain_blocks, FS, fs_size, distance)]
            )
            distance *= 2
        gain_full = jnp.concatenate(
            [
                lax.dynamic_index_in_dim(gain_blocks, own_fs ^ k, 0, keepdims=False)
                for k in range(fs_size)
            ],
            axis=1,
        ).astype(F32)
        full_gain_attn, full_gain_mlp = gain_full[0:1], gain_full[1:2]
        full_output = lax.all_gather(own_columns(w_output), FS, axis=0, tiled=True)
        out_cols = full_output.shape[1]
        output_rel = relative(full_output.reshape(seq_size, -1, out_cols))
        output_rel = output_rel.reshape(-1, out_cols)

        ff_rows = w_down.shape[0] // seq_size
        rows_in = w_gate.shape[0]

        def own_hidden(weight):
            shaped = weight.reshape(rows_in, fs_size, seq_size, ff_rows)
            part = lax.dynamic_index_in_dim(shaped, own_seq, 2, keepdims=False)
            return part.reshape(rows_in, pairs, 4, ff_rows)

        paired = jnp.stack([own_hidden(w_gate), own_hidden(w_up)], axis=1)
        paired = jnp.transpose(paired, (3, 0, 1, 2, 4))
        paired_send = jnp.stack(
            [
                jnp.stack([paired[:, :, :, k ^ p] for k in range(pairs)], axis=3)
                for p in range(pairs)
            ]
        ).reshape(fs_size, rows_in, -1)
        paired_full = lax.all_to_all(
            paired_send, FS, split_axis=0, concat_axis=0, tiled=True
        ).reshape(width, -1)
        down_own = lax.dynamic_slice_in_dim(w_down, own_seq * ff_rows, ff_rows, 0)
        down_full = jnp.concatenate(
            [down_own] + [swap(down_own, "p", pairs, k) for k in range(1, pairs)]
        )
        ff_own = ff_rows * pairs

        def gather_cube(block):
            beside = swap(block, "q", 2, 1)
            half = jnp.concatenate(gather_seq(block) + gather_seq(beside))
            return half, swap(half, "c", 2, 1)

        def scatter_cube(half, other):
            got = swap(low(other), "c", 2, 1)
            total = low(half + got.astype(F32)).reshape(2, seq_size, rows, width)
            across = scatter_seq([total[1, k] for k in range(seq_size)])
            back = swap(low(across), "q", 2, 1)
            return scatter_seq([total[0, k] for k in range(seq_size)]) + back.astype(F32)

        cot_halves = gather_cube(cot_own)

        sequence = jnp.concatenate(token_blocks).astype(F32)
        scale_one = norm_factor(sequence)
        normed_one = sequence * scale_one
        h_one = low(normed_one * full_gain_attn)
        order = relative(jnp.arange(length, dtype=jnp.int32).reshape(seq_size, rows)).reshape(-1)
        docs = relative(doc_ids.reshape(seq_size, rows)).reshape(-1)
        pos = relative(positions(doc_ids).reshape(seq_size, rows)).reshape(-1)
        cosine_table, sine_table = tables(pos)
        raw = product(h_one, full_qkv)
        group = q_cols // k_cols
        kv_heads = k_cols // HD
        queries = low(rotation(raw[:, :q_cols], cosine_table, sine_table))
        keys = low(rotation(raw[:, q_cols : q_cols + k_cols], cosine_table, sine_table))
        values = low(raw[:, q_cols + k_cols :])
        queries = queries.reshape(length, kv_heads, group, HD)
        keys = keys.reshape(length, kv_heads, HD)
        values = values.reshape(length, kv_heads, HD)
        visible = (order[None, :] <= order[:, None]) & (docs[None, :] == docs[:, None])
        factor = HD ** (-0.5)
        scores = jnp.einsum("qhgd,khd->hgqk", queries, keys, preferred_element_type=F32) * factor
        scores = jnp.where(visible[None, None], scores, NEGATIVE)
        largest = jnp.max(scores, axis=-1, keepdims=True)
        log_total = largest + jnp.log(jnp.sum(jnp.exp(scores - largest), axis=-1, keepdims=True))
        probs = jnp.exp(scores - log_total)
        probs_low = low(probs)
        mixed = low(
            jnp.einsum("hgqk,khd->qhgd", probs_low, values, preferred_element_type=F32)
        ).reshape(length, q_cols)
        def aligned(block, distance):
            parts = block.reshape(seq_size, rows, -1)
            return jnp.concatenate([parts[k ^ distance] for k in range(seq_size)])

        mixed_full = jnp.concatenate(
            [aligned(block, k) for k, block in enumerate(gather_seq(mixed))], axis=1
        )
        projected = product(mixed_full, output_rel).reshape(seq_size, rows, out_cols)

        def to_tokens(blocks):
            got = jnp.stack([blocks[0]] + [seq_swap(blocks[k], k) for k in range(1, seq_size)])
            return jnp.transpose(relative(got), (1, 0, 2)).reshape(rows, width)

        def to_columns(value):
            parts = [
                lax.dynamic_slice_in_dim(value, (own_seq ^ k) * out_cols, out_cols, 1)
                for k in range(seq_size)
            ]
            return jnp.concatenate(
                [parts[0]] + [seq_swap(parts[k], k) for k in range(1, seq_size)]
            )

        middle = tokens_own.astype(F32) + to_tokens(low(projected)).astype(F32)
        scale_two = norm_factor(middle)
        normed_two = middle * scale_two
        h_two = low(normed_two * full_gain_mlp)
        h_halves = gather_cube(h_two)

        outs, dhs, h_grads, down_grads = [], [], [], []
        for h_part, cot_part in zip(h_halves, cot_halves):
            both = product(h_part, paired_full)
            gate, upward = both[:, :ff_own], both[:, ff_own:]
            sigmoid_gate = jax.nn.sigmoid(gate)
            activated = gate * sigmoid_gate
            hidden = low(activated * upward)
            grad_hidden = product_back(cot_part, down_full)
            grad_up = low(grad_hidden * activated)
            grad_gate = low(
                grad_hidden * upward * sigmoid_gate * (1.0 + gate * (1.0 - sigmoid_gate))
            )
            grad_both = jnp.concatenate([grad_gate, grad_up], axis=1)
            dhs.append(product_back(grad_both, paired_full))
            outs.append(product(hidden, down_full))
            h_grads.append(outer_rows(h_part, grad_both))
            down_grads.append(outer_rows(hidden, cot_part))
        grad_normed_two = scatter_cube(*dhs)
        output = low(middle + scatter_cube(*outs))

        down_sum = (down_grads[0] + down_grads[1]).reshape(pairs, ff_rows, width)
        down_mine = down_sum[0]
        for k in range(1, pairs):
            down_mine = down_mine + swap(low(down_sum[k]), "p", pairs, k).astype(F32)
        down_out = lax.all_gather(low(down_mine), SEQ, axis=0, tiled=True).astype(F32)

        both_sum = low(h_grads[0] + h_grads[1]).reshape(fs_size, rows_in, -1)
        both_got = lax.all_to_all(both_sum, FS, split_axis=0, concat_axis=0, tiled=True)
        both_got = both_got.reshape(pairs, 4, rows_in, 2, pairs, ff_rows).astype(F32)
        both_mine = sum(
            jnp.stack([both_got[p, :, :, :, k ^ p] for k in range(pairs)]) for p in range(pairs)
        )
        both_mine = low(jnp.transpose(both_mine, (3, 2, 0, 1, 4)))
        both_out = lax.all_gather(both_mine, SEQ, axis=0)
        both_out = jnp.transpose(both_out, (1, 2, 3, 4, 0, 5)).reshape(2, rows_in, hidden_width)
        both_out = both_out.astype(F32)

        gain_two_grad = jnp.sum(grad_normed_two * normed_two, axis=0)
        grad_middle = cot_own.astype(F32) + norm_back(
            grad_normed_two * full_gain_mlp, normed_two, scale_two
        )
        middle_low = to_columns(low(grad_middle))
        grad_mixed = product_back(middle_low, output_rel).reshape(length, seq_size, q_cols)
        grad_heads = low(scatter_seq([aligned(grad_mixed[:, k], k) for k in range(seq_size)]))
        grad_heads = grad_heads.reshape(length, kv_heads, group, HD)
        grad_probs = jnp.einsum(
            "qhgd,khd->hgqk", grad_heads, values, preferred_element_type=F32
        )
        centre = jnp.sum(probs * grad_probs, axis=-1, keepdims=True)
        grad_scores = low(probs * (grad_probs - centre))
        query_grad = (
            jnp.einsum("hgqk,khd->qhgd", grad_scores, keys, preferred_element_type=F32) * factor
        )
        key_grad = (
            jnp.einsum("hgqk,qhgd->khd", grad_scores, queries, preferred_element_type=F32) * factor
        )
        value_grad = jnp.einsum(
            "hgqk,qhgd->khd", probs_low, grad_heads, preferred_element_type=F32
        )
        query_back = low(query_grad.reshape(length, -1)).astype(F32)
        key_back = low(key_grad.reshape(length, -1)).astype(F32)
        raw_grad = jnp.concatenate(
            [
                low(rotation(query_back, cosine_table, -sine_table)),
                low(rotation(key_back, cosine_table, -sine_table)),
                low(value_grad.reshape(length, -1)),
            ],
            axis=1,
        )
        grad_one_part = product_back(raw_grad, full_qkv)
        gain_one_grad = jnp.sum(grad_one_part * normed_one, axis=0)
        grad_normed_one = scatter_seq(
            [grad_one_part[k * rows : (k + 1) * rows] for k in range(seq_size)]
        )
        input_grad = grad_middle + norm_back(
            grad_normed_one * full_gain_attn, normed_one[:rows], scale_one[:rows]
        )
        output_grad = outer_rows(mixed_full, middle_low).reshape(seq_size, -1, out_cols)
        output_grad = relative(output_grad).reshape(width, out_cols)
        attn_grad = jnp.concatenate([outer_rows(h_one, raw_grad), output_grad], axis=1)
        attn_mine = lax.psum_scatter(low(attn_grad), FS, scatter_dimension=0, tiled=True)
        attn_out = lax.all_gather(attn_mine, SEQ, axis=0).astype(F32)

        def assembled(start, size):
            part = jnp.transpose(attn_out[:, :, start : start + size], (1, 0, 2))
            return part.reshape(rows_in, -1)

        gain_sums = sum_all(jnp.stack([gain_one_grad, gain_two_grad]))
        gain_mine = lax.dynamic_slice_in_dim(gain_sums, own_fs * rows_in, rows_in, 1)
        return (
            output.reshape(1, rows, width),
            low(input_grad).reshape(1, rows, width),
            assembled(0, q_cols),
            assembled(q_cols, k_cols),
            assembled(q_cols + k_cols, k_cols),
            assembled(q_cols + 2 * k_cols, out_cols),
            both_out[0],
            both_out[1],
            down_out,
            gain_mine[0],
            gain_mine[1],
        )

    return shards


def solution(mesh):
    seq_size, fs_size = mesh.shape["seq"], mesh.shape["fsdp"]
    fine = Mesh(
        mesh.devices.reshape(seq_size // 2, 2, fs_size // 4, 2, 2), SEQ + FS
    )
    token = P(FS, SEQ, None)
    weight = P(FS, None)
    gain = P(FS)
    return jax.shard_map(
        layer_step(seq_size, fs_size),
        mesh=fine,
        in_specs=(token, weight, token) + (weight,) * 7 + (gain, gain),
        out_specs=(token, token) + (weight,) * 7 + (gain, gain),
        check_vma=False,
    )
```
